512 devices in a mesh: depth: 64 (over y, z_lo, core), freq: 8 (over x, z_hi).
Axes of the slice: x: 4, y: 4, z: 16 (z_hi: 2, z_lo: 8; z = z_hi * 8 + z_lo), core: 2. Of those that a mesh axis runs over, the one named last changes fastest.
Arguments:
- extrapolation_operator: float32 [8, 64, 2, 512, 512], P('freq', 'depth'), may hold values from -0.1875 to 0.1875
- impedance_contrast: float32 [64, 512], P('depth'), may hold values from -3 to 3
- ascending_residual: float32 [8, 64, 5, 2, 96, 512], P('freq', 'depth'), may hold values from -6 to 6
- arriving_downward_matrices: float32 [8, 64, 2, 96, 512], P('freq', 'depth'), may hold values from -6 to 6
- shot_node_indices: int32 [4, 96], replicated, may hold values from 0 to 511
- emitted_pulse: float32 [8, 4, 2], P('freq'), may hold values from -4 to 4
Outputs:
- departing_downward_matrices: float32 [8, 64, 2, 96, 512], P('freq', 'depth')
- gradient: float32 [64, 512], P('depth', 'freq')
The draws below stay inside these ranges and needn't reach their ends.
All inputs are finite; a program needn't handle non-finite values.
Results may differ from the reference program's by a relative error of at most 0.00013.
Values sent between devices are 32-bit elements; how exact they have to be, the bound alone decides.
A program may use at most 64 MiB of HBM per device.

```python
import math
import jax
import jax.numpy as jnp
from jax import lax

HORIZONTAL_NODES = 512
SHOT_NUMBER = 96
TICKS = 5
STRATUM_NUMBER = 64
TEMPORAL_RATES = 8


def plant(drawn, stream_key, smallest, largest):
    longest = drawn.shape.index(max(drawn.shape))
    spots = []
    for shift in (0, 1):
        where = [jax.random.randint(jax.random.fold_in(stream_key, axis), (), 0, length) for axis, length in enumerate(drawn.shape)]
        where[longest] = (where[longest] + shift) % drawn.shape[longest]
        spots.append(tuple(where))
    return drawn.at[spots[0]].set(smallest).at[spots[1]].set(largest)


def steps_of(key, extent, split, smallest, high):
    factor_of = 1.0
    for position, shards_of in split:
        draws = jax.random.uniform(jax.random.fold_in(jax.random.fold_in(key, 6), position), (shards_of,), jnp.float32, smallest / len(split), high / len(split))
        factor_of = factor_of * jnp.repeat(jnp.exp(draws), extent[position] // shards_of).reshape((-1,) + (1,) * (len(extent) - 1 - position))
    return factor_of


def bell_draw(stream_key, dims, scale, limit, shards=(), kind=jnp.bfloat16):
    array = scale * jax.random.normal(stream_key, dims, jnp.float32)
    if shards:
        array = array * steps_of(stream_key, dims, shards, -0.22, 0.18)
    return jnp.clip(array, -limit, limit).astype(kind)


def setup_inputs(seed: int = 0) -> dict:
    key_of = jax.random.split(jax.random.key(seed), 7)
    return {
        "extrapolation_operator": bell_draw(key_of[0], (TEMPORAL_RATES, STRATUM_NUMBER, 2, HORIZONTAL_NODES, HORIZONTAL_NODES), (2 * HORIZONTAL_NODES) ** -0.5, 0.1875, ((0, 8), (1, 64)), jnp.float32),
        "impedance_contrast": bell_draw(key_of[1], (STRATUM_NUMBER, HORIZONTAL_NODES), 0.5, 3.0, ((0, 64),), jnp.float32),
        "ascending_residual": bell_draw(key_of[2], (TEMPORAL_RATES, STRATUM_NUMBER, TICKS, 2, SHOT_NUMBER, HORIZONTAL_NODES), 1.0, 6.0, ((0, 8), (1, 64)), jnp.float32),
        "arriving_downward_matrices": bell_draw(key_of[3], (TEMPORAL_RATES, STRATUM_NUMBER, 2, SHOT_NUMBER, HORIZONTAL_NODES), 1.0, 6.0, ((0, 8), (1, 64)), jnp.float32),
        "shot_node_indices": plant(jax.random.randint(key_of[4], (TICKS - 1, SHOT_NUMBER), 0, HORIZONTAL_NODES), jax.random.fold_in(key_of[4], 1), 0, HORIZONTAL_NODES - 1).astype(jnp.int32),
        "emitted_pulse": bell_draw(key_of[5], (TEMPORAL_RATES, TICKS - 1, 2), 1.0, 4.0, ((0, 8),), jnp.float32),
    }


def complex_step(mixed, prop_parts):
    highest = lax.Precision.HIGHEST

    def product(left, right):
        return jnp.einsum('zsy,zyx->zsx', left, right, precision=highest)
    real_out = product(mixed[:, 0], prop_parts[:, 0]) - product(mixed[:, 1], prop_parts[:, 1])
    imag_out = product(mixed[:, 0], prop_parts[:, 1]) + product(mixed[:, 1], prop_parts[:, 0])
    return jnp.stack([real_out, imag_out], 1)

def inject_panel(wave_pair, source_sites):
    columns = jnp.arange(HORIZONTAL_NODES, dtype=jnp.int32)
    hits = (columns[None, :] == source_sites[:, None].astype(jnp.int32)).astype(jnp.float32)
    return wave_pair[:, None, None] * hits[None]

def reference(extrapolation_operator, impedance_contrast, ascending_residual, arriving_downward_matrices, shot_node_indices, emitted_pulse):

    def chosen_temporal_rate(operand_list):
        propagator_field, upgoing_field, transit_field, wavelet_spectrum = operand_list
        present_shot_matrix = transit_field
        gradient_sum = jnp.zeros((STRATUM_NUMBER, HORIZONTAL_NODES), jnp.float32)
        outgoing = present_shot_matrix
        for moment in range(TICKS):
            wave_now = upgoing_field[:, moment]
            gradient_sum = gradient_sum + lax.optimization_barrier(jnp.sum(present_shot_matrix * wave_now, axis=(1, 2)))
            mixed = present_shot_matrix + impedance_contrast[:, None, None, :] * wave_now
            outgoing = complex_step(mixed, propagator_field)
            if moment < TICKS - 1:
                top_panel = inject_panel(wavelet_spectrum[moment], shot_node_indices[moment])
                present_shot_matrix = jnp.concatenate([top_panel[None], outgoing[:-1]], 0)
        return (outgoing, gradient_sum / math.sqrt(SHOT_NUMBER * TICKS))
    departing_downward_matrices, reflector_sensitivity_shares = lax.map(chosen_temporal_rate, (extrapolation_operator, ascending_residual, arriving_downward_matrices, emitted_pulse))
    return (departing_downward_matrices, lax.optimization_barrier(jnp.sum(reflector_sensitivity_shares, 0)))
```

```python
import functools
import math

import jax
import jax.numpy as jnp
from jax import lax
from jax.experimental import pallas as pl
from jax.experimental.pallas import tpu as pltpu
from jax.sharding import PartitionSpec as P

TICKS = 5
MESH = pl.DeviceIdType.MESH


def kernel(
    levels,
    rates,
    parts,
    prop_hbm,
    refl_hbm,
    asc_hbm,
    first_hbm,
    spots_hbm,
    pulse_hbm,
    leaving_ref,
    grad_ref,
    prop,
    high,
    low,
    refl,
    asc,
    arriving,
    outgoing,
    spots,
    pulse,
    total,
    shares,
    load_sem,
    send_sem,
    recv_sem,
    give_sem,
    take_sem,
):
    level = lax.axis_index("depth")
    rate = lax.axis_index("freq")
    shots, nodes = arriving.shape[2], arriving.shape[3]
    rows = shots // parts

    loads = [
        pltpu.make_async_copy(prop_hbm, prop, load_sem.at[0]),
        pltpu.make_async_copy(first_hbm, arriving.at[0], load_sem.at[1]),
        pltpu.make_async_copy(refl_hbm, refl, load_sem.at[2]),
        pltpu.make_async_copy(spots_hbm, spots, load_sem.at[3]),
        pltpu.make_async_copy(pulse_hbm, pulse, load_sem.at[4]),
    ]
    waves = [pltpu.make_async_copy(asc_hbm.at[t], asc.at[t], load_sem.at[5 + t]) for t in range(TICKS)]
    loads[0].start()
    loads[1].start()
    waves[0].start()
    for load in loads[2:]:
        load.start()
    for wave in waves[1:]:
        wave.start()

    barrier = pltpu.get_barrier_semaphore()

    @pl.when(level > 0)
    def _():
        pl.semaphore_signal(barrier, inc=1, device_id={"depth": level - 1}, device_id_type=MESH)

    for away in range(1, rates):
        pl.semaphore_signal(barrier, inc=1, device_id={"freq": lax.rem(rate + away, rates)}, device_id_type=MESH)

    for load in loads:
        load.wait()

    for part in range(2):
        whole = prop[part]
        top = whole.astype(jnp.bfloat16)
        high[:, part * nodes : (part + 1) * nodes] = top
        low[:, part * nodes : (part + 1) * nodes] = (whole - top.astype(jnp.float32)).astype(jnp.bfloat16)

    @pl.when(level == 0)
    def _():
        column = lax.broadcasted_iota(jnp.int32, (shots, nodes), 1)
        turned = jnp.transpose(spots[...].astype(jnp.float32)).astype(jnp.int32)
        for t in range(TICKS - 1):
            hit = (column == turned[:, t : t + 1]).astype(jnp.float32)
            arriving[t + 1, 0] = hit * pulse[t : t + 1, 0:1]
            arriving[t + 1, 1] = hit * pulse[t : t + 1, 1:2]

    @pl.when(level < levels - 1)
    def _():
        pl.semaphore_wait(barrier, rates)

    @pl.when(level == levels - 1)
    def _():
        pl.semaphore_wait(barrier, rates - 1)

    total[...] = jnp.zeros_like(total)

    def passing(t, c):
        return pltpu.make_async_remote_copy(
            src_ref=outgoing.at[t, :, pl.ds(c * rows, rows)],
            dst_ref=arriving.at[t + 1, :, pl.ds(c * rows, rows)],
            send_sem=send_sem.at[t, c],
            recv_sem=recv_sem.at[t, c],
            device_id={"depth": lax.rem(level + 1, levels)},
            device_id_type=MESH,
        )

    for t in range(TICKS):
        if t > 0:
            waves[t].wait()
        else:
            waves[0].wait()
        for c in range(parts):
            at = pl.ds(c * rows, rows)
            if t > 0:

                @pl.when(level > 0)
                def _():
                    passing(t - 1, c).wait_recv()

            here = arriving[t, :, at]
            rising = asc[t, :, at]
            total[...] += jnp.sum((here * rising).reshape(2 * rows // 8, 8, nodes), axis=0)
            mixed = (here + refl[...] * rising).reshape(2 * rows, nodes)
            top = mixed.astype(jnp.bfloat16)
            rest = (mixed - top.astype(jnp.float32)).astype(jnp.bfloat16)
            both = jnp.concatenate([top, rest], axis=0)
            wide = jnp.dot(both, high[...], preferred_element_type=jnp.float32)
            wide = wide[: 2 * rows] + wide[2 * rows :] + jnp.dot(top, low[...], preferred_element_type=jnp.float32)
            real = wide[:rows, :nodes] - wide[rows:, nodes:]
            imag = wide[:rows, nodes:] + wide[rows:, :nodes]
            if t < TICKS - 1:
                outgoing[t, 0, at] = real
                outgoing[t, 1, at] = imag

                @pl.when(level < levels - 1)
                def _():
                    passing(t, c).start()
            else:
                leaving_ref[0, at] = real
                leaving_ref[1, at] = imag

    half = nodes // rates
    per = 128 // half
    for tile in range(nodes // 128):
        shares[rates + tile] = total[:, tile * 128 : (tile + 1) * 128]

    def give(away):
        other = lax.rem(rate + away, rates)
        return pltpu.make_async_remote_copy(
            src_ref=shares.at[rates + other // per],
            dst_ref=shares.at[away],
            send_sem=give_sem.at[away],
            recv_sem=take_sem.at[away],
            device_id={"freq": other},
            device_id_type=MESH,
        )

    for away in range(1, rates):
        give(away).start()
    summed = shares[rates + rate // per]
    for away in range(1, rates):
        give(away).wait_recv()
        summed += shares[away]
    row = jnp.sum(summed, axis=0, keepdims=True) * (1.0 / math.sqrt(shots * TICKS))
    place = lax.rem(rate, per)
    mine = row[:, :half]
    for k in range(1, per):
        mine = jnp.where(place == k, row[:, k * half : (k + 1) * half], mine)
    grad_ref[...] = mine
    for away in range(1, rates):
        give(away).wait_send()

    @pl.when(level < levels - 1)
    def _():
        for t in range(TICKS - 1):
            for c in range(parts):
                passing(t, c).wait_send()


def local(levels, rates, prop, refl, asc, first, spots, pulse):
    shots, nodes = first.shape[3], first.shape[4]
    parts = 3
    prop = prop.reshape(2, nodes, nodes)
    asc = asc.reshape(TICKS, 2, shots, nodes)
    first = first.reshape(2, shots, nodes)
    pulse = pulse.reshape(TICKS - 1, 2)
    leaving, grad = pl.pallas_call(
        functools.partial(kernel, levels, rates, parts),
        out_shape=(
            jax.ShapeDtypeStruct((2, shots, nodes), jnp.float32),
            jax.ShapeDtypeStruct((1, nodes // rates), jnp.float32),
        ),
        in_specs=[pl.BlockSpec(memory_space=pl.ANY)] * 6,
        out_specs=(pl.BlockSpec(memory_space=pltpu.VMEM), pl.BlockSpec(memory_space=pltpu.VMEM)),
        scratch_shapes=[
            pltpu.VMEM((2, nodes, nodes), jnp.float32),
            pltpu.VMEM((nodes, 2 * nodes), jnp.bfloat16),
            pltpu.VMEM((nodes, 2 * nodes), jnp.bfloat16),
            pltpu.VMEM((1, nodes), jnp.float32),
            pltpu.VMEM((TICKS, 2, shots, nodes), jnp.float32),
            pltpu.VMEM((TICKS, 2, shots, nodes), jnp.float32),
            pltpu.VMEM((TICKS - 1, 2, shots, nodes), jnp.float32),
            pltpu.VMEM((TICKS - 1, shots), jnp.int32),
            pltpu.VMEM((TICKS - 1, 2), jnp.float32),
            pltpu.VMEM((8, nodes), jnp.float32),
            pltpu.VMEM((rates + nodes // 128, 8, 128), jnp.float32),
            pltpu.SemaphoreType.DMA((5 + TICKS,)),
            pltpu.SemaphoreType.DMA((TICKS - 1, parts)),
            pltpu.SemaphoreType.DMA((TICKS - 1, parts)),
            pltpu.SemaphoreType.DMA((rates,)),
            pltpu.SemaphoreType.DMA((rates,)),
        ],
        compiler_params=pltpu.CompilerParams(collective_id=0, has_side_effects=True, vmem_limit_bytes=48 << 20),
    )(prop, refl, asc, first, spots, pulse)
    return leaving[None, None], grad


def solution(mesh):
    placed = (
        P("freq", "depth", None, None, None),
        P("depth", None),
        P("freq", "depth", None, None, None, None),
        P("freq", "depth", None, None, None),
        P(),
        P("freq", None, None),
    )
    return jax.shard_map(
        functools.partial(local, mesh.shape["depth"], mesh.shape["freq"]),
        mesh=mesh,
        in_specs=placed,
        out_specs=(P("freq", "depth", None, None, None), P("depth", "freq")),
        check_vma=False,
    )
```

```python
import functools
import math

import jax
import jax.numpy as jnp
from jax import lax
from jax.experimental import pallas as pl
from jax.experimental.pallas import tpu as pltpu
from jax.sharding import PartitionSpec as P

TICKS = 5
MESH = pl.DeviceIdType.MESH


def kernel(
    levels,
    rates,
    parts,
    prop_hbm,
    refl_hbm,
    asc_hbm,
    first_hbm,
    spots_hbm,
    pulse,
    leaving_ref,
    grad_ref,
    prop,
    high,
    low,
    refl,
    asc,
    arriving,
    outgoing,
    spots,
    total,
    shares,
    load_sem,
    send_sem,
    recv_sem,
    give_sem,
    take_sem,
):
    level = lax.axis_index("depth")
    rate = lax.axis_index("freq")
    shots, nodes = arriving.shape[2], arriving.shape[3]
    rows = shots // parts

    loads = [
        pltpu.make_async_copy(prop_hbm, prop, load_sem.at[0]),
        pltpu.make_async_copy(first_hbm, arriving.at[0], load_sem.at[1]),
        pltpu.make_async_copy(refl_hbm, refl, load_sem.at[2]),
        pltpu.make_async_copy(spots_hbm, spots, load_sem.at[3]),
    ]
    waves = [pltpu.make_async_copy(asc_hbm.at[t], asc.at[t], load_sem.at[5 + t]) for t in range(TICKS)]
    loads[0].start()
    loads[1].start()
    waves[0].start()
    for load in loads[2:]:
        load.start()
    for wave in waves[1:]:
        wave.start()

    barrier = pltpu.get_barrier_semaphore()

    @pl.when(level > 0)
    def _():
        pl.semaphore_signal(barrier, inc=1, device_id={"depth": level - 1}, device_id_type=MESH)

    for away in range(1, rates):
        pl.semaphore_signal(barrier, inc=1, device_id={"freq": lax.rem(rate + away, rates)}, device_id_type=MESH)

    for load in loads:
        load.wait()

    for part in range(2):
        whole = prop[part]
        top = whole.astype(jnp.bfloat16)
        high[:, part * nodes : (part + 1) * nodes] = top
        low[:, part * nodes : (part + 1) * nodes] = (whole - top.astype(jnp.float32)).astype(jnp.bfloat16)

    @pl.when(level == 0)
    def _():
        column = lax.broadcasted_iota(jnp.int32, (shots, nodes), 1)
        turned = jnp.transpose(spots[...].astype(jnp.float32)).astype(jnp.int32)
        for t in range(TICKS - 1):
            hit = (column == turned[:, t : t + 1]).astype(jnp.float32)
            arriving[t + 1, 0] = hit * pulse[0:1, t : t + 1]
            arriving[t + 1, 1] = hit * pulse[1:2, t : t + 1]

    @pl.when(level < levels - 1)
    def _():
        pl.semaphore_wait(barrier, rates)

    @pl.when(level == levels - 1)
    def _():
        pl.semaphore_wait(barrier, rates - 1)

    total[...] = jnp.zeros_like(total)

    def passing(t, c):
        return pltpu.make_async_remote_copy(
            src_ref=outgoing.at[t, :, pl.ds(c * rows, rows)],
            dst_ref=arriving.at[t + 1, :, pl.ds(c * rows, rows)],
            send_sem=send_sem.at[t, c],
            recv_sem=recv_sem.at[t, c],
            device_id={"depth": lax.rem(level + 1, levels)},
            device_id_type=MESH,
        )

    for t in range(TICKS):
        if t > 0:
            waves[t].wait()
        else:
            waves[0].wait()
        for c in range(parts):
            at = pl.ds(c * rows, rows)
            if t > 0:

                @pl.when(level > 0)
                def _():
                    passing(t - 1, c).wait_recv()

            here = arriving[t, :, at]
            rising = asc[t, :, at]
            total[...] += jnp.sum((here * rising).reshape(2 * rows // 8, 8, nodes), axis=0)
            mixed = (here + refl[...] * rising).reshape(2 * rows, nodes)
            top = mixed.astype(jnp.bfloat16)
            rest = (mixed - top.astype(jnp.float32)).astype(jnp.bfloat16)
            both = jnp.concatenate([top, rest], axis=0)
            wide = jnp.dot(both, high[...], preferred_element_type=jnp.float32)
            wide = wide[: 2 * rows] + wide[2 * rows :] + jnp.dot(top, low[...], preferred_element_type=jnp.float32)
            real = wide[:rows, :nodes] - wide[rows:, nodes:]
            imag = wide[:rows, nodes:] + wide[rows:, :nodes]
            if t < TICKS - 1:
                outgoing[t, 0, at] = real
                outgoing[t, 1, at] = imag

                @pl.when(level < levels - 1)
                def _():
                    passing(t, c).start()
            else:
                leaving_ref[0, at] = real
                leaving_ref[1, at] = imag

    half = nodes // rates
    per = 128 // half
    for tile in range(nodes // 128):
        shares[rates + tile] = total[:, tile * 128 : (tile + 1) * 128]

    def give(away):
        other = lax.rem(rate + away, rates)
        return pltpu.make_async_remote_copy(
            src_ref=shares.at[rates + other // per],
            dst_ref=shares.at[away],
            send_sem=give_sem.at[away],
            recv_sem=take_sem.at[away],
            device_id={"freq": other},
            device_id_type=MESH,
        )

    for away in range(1, rates):
        give(away).start()
    summed = shares[rates + rate // per]
    for away in range(1, rates):
        give(away).wait_recv()
        summed += shares[away]
    row = jnp.sum(summed, axis=0, keepdims=True) * (1.0 / math.sqrt(shots * TICKS))
    place = lax.rem(rate, per)
    mine = row[:, :half]
    for k in range(1, per):
        mine = jnp.where(place == k, row[:, k * half : (k + 1) * half], mine)
    grad_ref[...] = mine
    for away in range(1, rates):
        give(away).wait_send()

    @pl.when(level < levels - 1)
    def _():
        for t in range(TICKS - 1):
            for c in range(parts):
                passing(t, c).wait_send()


def local(levels, rates, prop, refl, asc, first, spots, pulse):
    shots, nodes = first.shape[3], first.shape[4]
    parts = 3
    prop = prop.reshape(2, nodes, nodes)
    asc = asc.reshape(TICKS, 2, shots, nodes)
    first = first.reshape(2, shots, nodes)
    pulse = pulse.reshape(TICKS - 1, 2).T
    leaving, grad = pl.pallas_call(
        functools.partial(kernel, levels, rates, parts),
        out_shape=(
            jax.ShapeDtypeStruct((2, shots, nodes), jnp.float32),
            jax.ShapeDtypeStruct((1, nodes // rates), jnp.float32),
        ),
        in_specs=[pl.BlockSpec(memory_space=pltpu.HBM)] * 5 + [pl.BlockSpec(memory_space=pltpu.VMEM)],
        out_specs=(pl.BlockSpec(memory_space=pltpu.VMEM), pl.BlockSpec(memory_space=pltpu.VMEM)),
        scratch_shapes=[
            pltpu.VMEM((2, nodes, nodes), jnp.float32),
            pltpu.VMEM((nodes, 2 * nodes), jnp.bfloat16),
            pltpu.VMEM((nodes, 2 * nodes), jnp.bfloat16),
            pltpu.VMEM((1, nodes), jnp.float32),
            pltpu.VMEM((TICKS, 2, shots, nodes), jnp.float32),
            pltpu.VMEM((TICKS, 2, shots, nodes), jnp.float32),
            pltpu.VMEM((TICKS - 1, 2, shots, nodes), jnp.float32),
            pltpu.VMEM((TICKS - 1, shots), jnp.int32),
            pltpu.VMEM((8, nodes), jnp.float32),
            pltpu.VMEM((rates + nodes // 128, 8, 128), jnp.float32),
            pltpu.SemaphoreType.DMA((5 + TICKS,)),
            pltpu.SemaphoreType.DMA((TICKS - 1, parts)),
            pltpu.SemaphoreType.DMA((TICKS - 1, parts)),
            pltpu.SemaphoreType.DMA((rates,)),
            pltpu.SemaphoreType.DMA((rates,)),
        ],
        compiler_params=pltpu.CompilerParams(collective_id=0, has_side_effects=True),
    )(prop, refl, asc, first, spots, pulse)
    return leaving[None, None], grad


def solution(mesh):
    placed = (
        P("freq", "depth", None, None, None),
        P("depth", None),
        P("freq", "depth", None, None, None, None),
        P("freq", "depth", None, None, None),
        P(),
        P("freq", None, None),
    )
    return jax.shard_map(
        functools.partial(local, mesh.shape["depth"], mesh.shape["freq"]),
        mesh=mesh,
        in_specs=placed,
        out_specs=(P("freq", "depth", None, None, None), P("depth", "freq")),
        check_vma=False,
    )
```

```python
import functools
import math

import jax
import jax.numpy as jnp
from jax import lax
from jax.experimental import pallas as pl
from jax.experimental.pallas import tpu as pltpu
from jax.sharding import PartitionSpec as P

TICKS = 5
RUN = 16
PIECES = 4
MESH = pl.DeviceIdType.MESH


def kernel(
    levels,
    rates,
    parts,
    prop_hbm,
    refl_hbm,
    asc_hbm,
    first_hbm,
    spots_hbm,
    pulse,
    leaving_ref,
    grad_ref,
    prop,
    high,
    low,
    refl,
    asc,
    arriving,
    outgoing,
    passed,
    spots,
    total,
    shares,
    load_sem,
    wave_sem,
    block_sem,
    send_sem,
    recv_sem,
    give_sem,
    take_sem,
    go_sem,
    land_sem,
    onward_sem,
):
    level = lax.axis_index("depth")
    rate = lax.axis_index("freq")
    last = levels - 1
    shots, nodes = arriving.shape[2], arriving.shape[3]
    rows = shots // parts
    blocks = block_sem.shape[0]
    deep = nodes // blocks

    def block_load(k):
        return pltpu.make_async_copy(prop_hbm.at[:, pl.ds(k * deep, deep)], prop.at[:, pl.ds(k * deep, deep)], block_sem.at[k])

    def wave_load(t):
        return pltpu.make_async_copy(asc_hbm.at[t], asc.at[t], wave_sem.at[t])

    loads = [
        pltpu.make_async_copy(refl_hbm, refl, load_sem.at[0]),
        pltpu.make_async_copy(first_hbm, arriving.at[0], load_sem.at[1]),
        pltpu.make_async_copy(spots_hbm, spots, load_sem.at[2]),
    ]
    barrier = pltpu.get_barrier_semaphore()

    line, spot = level // RUN, lax.rem(level, RUN)
    lines = levels // RUN
    first = (spot == 0) & (level > 0)
    long = (spot == RUN - 1) & (level < last)
    near = (spot == RUN // 2) & (line < lines - 1)
    side = (spot == RUN - 2) & (line > 0)
    plain = (level < last) & (spot != RUN - 1)

    def ready(there):
        pl.semaphore_signal(barrier, inc=1, device_id={"depth": there}, device_id_type=MESH)

    @pl.when(spot > 0)
    def _():
        ready(level - 1)

    @pl.when(first)
    def _():
        ready(level - RUN // 2)
        ready(level + RUN - 2)

    @pl.when(near)
    def _():
        ready(level + RUN // 2 - 1)

    @pl.when(side)
    def _():
        ready(level - RUN + 1)

    for k in range(blocks):
        block_load(k).start()
    for load in loads:
        load.start()
    wave_load(0).start()

    home = lax.rem(level, rates)
    hub = level == last
    inside = hub & (home == rate)

    @pl.when(jnp.logical_not(inside))
    def _():
        pl.semaphore_signal(barrier, inc=1, device_id={"depth": last, "freq": home}, device_id_type=MESH)

    for k in range(blocks):
        block_load(k).wait()
        at = pl.ds(k * deep, deep)
        for part in range(2):
            whole = prop[part, at]
            top = whole.astype(jnp.bfloat16)
            high[at, part * nodes : (part + 1) * nodes] = top
            low[at, part * nodes : (part + 1) * nodes] = (whole - top.astype(jnp.float32)).astype(jnp.bfloat16)
    for load in loads:
        load.wait()
    wave_load(0).wait()
    for t in range(1, TICKS):
        wave_load(t).start()

    total[...] = jnp.zeros_like(total)

    def admit():
        @pl.when(level < last)
        def _():
            pl.semaphore_wait(barrier, 1 + jnp.where(long | near | side, 1, 0))

        @pl.when(hub)
        def _():
            pl.semaphore_wait(barrier, levels - jnp.where(inside, 1, 0))

            def release(i, carry):
                there, which = (i // rates) * rates + rate, lax.rem(i, rates)

                @pl.when(jnp.logical_or(there != level, which != rate))
                def _():
                    pl.semaphore_signal(go_sem, inc=1, device_id={"depth": there, "freq": which}, device_id_type=MESH)

                return carry

            lax.fori_loop(0, levels, release, 0)

    def passing(t, c):
        return pltpu.make_async_remote_copy(
            src_ref=outgoing.at[t, :, pl.ds(c * rows, rows)],
            dst_ref=arriving.at[t + 1, :, pl.ds(c * rows, rows)],
            send_sem=send_sem.at[t, c],
            recv_sem=recv_sem.at[t, c],
            device_id={"depth": lax.rem(level + 1, levels)},
            device_id_type=MESH,
        )

    size = rows // PIECES

    def share(which):
        return lines - 1 - which

    def piece(t, c, p):
        at = pl.ds(c * rows + p * size, size)
        return pltpu.make_async_remote_copy(
            src_ref=outgoing.at[t, :, at],
            dst_ref=passed.at[t, :, at],
            send_sem=send_sem.at[t, c],
            recv_sem=land_sem.at[t, c, p],
            device_id={"depth": jnp.where(long, jnp.where(p < share(line), level - RUN // 2 + 1, level + RUN - 1), level)},
            device_id_type=MESH,
        )

    def onward(t, c, p):
        at = pl.ds(c * rows + p * size, size)
        return pltpu.make_async_remote_copy(
            src_ref=passed.at[t, :, at],
            dst_ref=arriving.at[t + 1, :, at],
            send_sem=onward_sem.at[t, c, p],
            recv_sem=recv_sem.at[t, c],
            device_id={"depth": jnp.where(near, level + RUN // 2, jnp.where(side, level - RUN + 2, level))},
            device_id_type=MESH,
        )

    def carried(p):
        return (near & (p < share(line))) | (side & (p >= share(line - 1)))

    def send(t, c):
        @pl.when(plain)
        def _():
            passing(t, c).start()

        @pl.when(long)
        def _():
            for p in range(PIECES):
                piece(t, c, p).start()

    def relay(t, c):
        @pl.when(near | side)
        def _():
            for p in range(PIECES):

                @pl.when(carried(p))
                def _():
                    piece(t, c, p).wait_recv()
                    onward(t, c, p).start()

    def arrive(t, c):
        if t > 0:

            @pl.when(level > 0)
            def _():
                passing(t - 1, c).wait_recv()

    def correlate(t, c):
        at = pl.ds(c * rows, rows)
        total[...] += jnp.sum((arriving[t, :, at] * asc[t, :, at]).reshape(2 * rows // 8, 8, nodes), axis=0)

    def propagate(t, c):
        at = pl.ds(c * rows, rows)
        mixed = (arriving[t, :, at] + refl[...] * asc[t, :, at]).reshape(2 * rows, nodes)
        top = mixed.astype(jnp.bfloat16)
        rest = (mixed - top.astype(jnp.float32)).astype(jnp.bfloat16)
        both = jnp.concatenate([top, rest], axis=0)
        wide = jnp.dot(both, high[...], preferred_element_type=jnp.float32)
        wide = wide[: 2 * rows] + wide[2 * rows :] + jnp.dot(top, low[...], preferred_element_type=jnp.float32)
        result = outgoing.at[t] if t < TICKS - 1 else leaving_ref
        result[0, at] = wide[:rows, :nodes] - wide[rows:, nodes:]
        result[1, at] = wide[:rows, nodes:] + wide[rows:, :nodes]

    for c in range(parts):
        propagate(0, c)
        if c == 0:
            admit()
        send(0, c)
        correlate(0, c)

    for t in range(TICKS - 1):
        if t > 0:
            wave_load(t).wait()
        for c in range(parts if t > 0 else 0):
            arrive(t, c)
            propagate(t, c)
            send(t, c)
            correlate(t, c)
            if t == 1:
                relay(0, c)
            if t > 1:
                relay(t, c)
        if t == 1:
            for c in range(parts):
                relay(1, c)
        if t == 0:

            @pl.when(level == 0)
            def _():
                column = lax.broadcasted_iota(jnp.int32, (shots, nodes), 1)
                turned = jnp.transpose(spots[...].astype(jnp.float32)).astype(jnp.int32)
                for u in range(TICKS - 1):
                    hit = (column == turned[:, u : u + 1]).astype(jnp.float32)
                    arriving[u + 1, 0] = hit * pulse[0:1, u : u + 1]
                    arriving[u + 1, 1] = hit * pulse[1:2, u : u + 1]

    t = TICKS - 1
    wave_load(t).wait()
    for c in range(parts - 1):
        arrive(t, c)
        correlate(t, c)
        propagate(t, c)
    arrive(t, parts - 1)
    correlate(t, parts - 1)

    half = nodes // rates
    per = 128 // half
    for tile in range(nodes // 128):
        shares[rates + tile] = total[:, tile * 128 : (tile + 1) * 128]

    def give(away):
        other = lax.rem(rate + away, rates)
        return pltpu.make_async_remote_copy(
            src_ref=shares.at[rates + other // per],
            dst_ref=shares.at[away],
            send_sem=give_sem.at[away],
            recv_sem=take_sem.at[away],
            device_id={"freq": other},
            device_id_type=MESH,
        )

    @pl.when(jnp.logical_not(inside))
    def _():
        pl.semaphore_wait(go_sem, 1)

    for away in range(1, rates):
        give(away).start()

    propagate(t, parts - 1)

    @pl.when(level < last)
    def _():
        for u in range(TICKS - 1):
            for c in range(parts):
                passing(u, c).wait_send()

    @pl.when(near | side)
    def _():
        for p in range(PIECES):

            @pl.when(carried(p))
            def _():
                for u in range(TICKS - 1):
                    for c in range(parts):
                        onward(u, c, p).wait_send()

    summed = shares[rates + rate // per]
    for away in range(1, rates):
        give(away).wait_recv()
        summed += shares[away]
    row = jnp.sum(summed, axis=0, keepdims=True) * (1.0 / math.sqrt(shots * TICKS))
    place = lax.rem(rate, per)
    mine = row[:, :half]
    for k in range(1, per):
        mine = jnp.where(place == k, row[:, k * half : (k + 1) * half], mine)
    grad_ref[...] = mine
    for away in range(1, rates):
        give(away).wait_send()


def local(levels, rates, prop, refl, asc, first, spots, pulse):
    shots, nodes = first.shape[3], first.shape[4]
    parts = 3
    prop = prop.reshape(2, nodes, nodes)
    asc = asc.reshape(TICKS, 2, shots, nodes)
    first = first.reshape(2, shots, nodes)
    pulse = pulse.reshape(TICKS - 1, 2).T
    prop, refl, asc, first, spots, pulse = (pltpu.with_memory_space_constraint(x, pltpu.HBM) for x in (prop, refl, asc, first, spots, pulse))
    leaving, grad = pl.pallas_call(
        functools.partial(kernel, levels, rates, parts),
        out_shape=(
            jax.ShapeDtypeStruct((2, shots, nodes), jnp.float32),
            jax.ShapeDtypeStruct((1, nodes // rates), jnp.float32),
        ),
        in_specs=[pl.BlockSpec(memory_space=pltpu.HBM)] * 5 + [pl.BlockSpec(memory_space=pltpu.VMEM)],
        out_specs=(pl.BlockSpec(memory_space=pltpu.VMEM), pl.BlockSpec(memory_space=pltpu.VMEM)),
        scratch_shapes=[
            pltpu.VMEM((2, nodes, nodes), jnp.float32),
            pltpu.VMEM((nodes, 2 * nodes), jnp.bfloat16),
            pltpu.VMEM((nodes, 2 * nodes), jnp.bfloat16),
            pltpu.VMEM((1, nodes), jnp.float32),
            pltpu.VMEM((TICKS, 2, shots, nodes), jnp.float32),
            pltpu.VMEM((TICKS, 2, shots, nodes), jnp.float32),
            pltpu.VMEM((TICKS - 1, 2, shots, nodes), jnp.float32),
            pltpu.VMEM((TICKS - 1, 2, shots, nodes), jnp.float32),
            pltpu.VMEM((TICKS - 1, shots), jnp.int32),
            pltpu.VMEM((8, nodes), jnp.float32),
            pltpu.VMEM((rates + nodes // 128, 8, 128), jnp.float32),
            pltpu.SemaphoreType.DMA((3,)),
            pltpu.SemaphoreType.DMA((TICKS,)),
            pltpu.SemaphoreType.DMA((4,)),
            pltpu.SemaphoreType.DMA((TICKS - 1, parts)),
            pltpu.SemaphoreType.DMA((TICKS - 1, parts)),
            pltpu.SemaphoreType.DMA((rates,)),
            pltpu.SemaphoreType.DMA((rates,)),
            pltpu.SemaphoreType.REGULAR,
            pltpu.SemaphoreType.DMA((TICKS - 1, parts, PIECES)),
            pltpu.SemaphoreType.DMA((TICKS - 1, parts, PIECES)),
        ],
        compiler_params=pltpu.CompilerParams(collective_id=0, has_side_effects=True, vmem_limit_bytes=32 << 20),
    )(prop, refl, asc, first, spots, pulse)
    return leaving[None, None], grad


def solution(mesh):
    placed = (
        P("freq", "depth", None, None, None),
        P("depth", None),
        P("freq", "depth", None, None, None, None),
        P("freq", "depth", None, None, None),
        P(),
        P("freq", None, None),
    )
    return jax.shard_map(
        functools.partial(local, mesh.shape["depth"], mesh.shape["freq"]),
        mesh=mesh,
        in_specs=placed,
        out_specs=(P("freq", "depth", None, None, None), P("depth", "freq")),
        check_vma=False,
    )
```

```python
import functools
import math

import jax
import jax.numpy as jnp
from jax import lax
from jax.experimental import pallas as pl
from jax.experimental.pallas import tpu as pltpu
from jax.sharding import PartitionSpec as P

TICKS = 5
RUN = 16
NEAR = 10
SHARES = ((4, 3, 2), (3, 2, 1), (3, 2, 1), (2, 1, 1))
PIECES = 4
MESH = pl.DeviceIdType.MESH


def kernel(
    levels,
    rates,
    parts,
    prop_hbm,
    refl_hbm,
    asc_hbm,
    first_hbm,
    spots_hbm,
    pulse,
    leaving_ref,
    grad_ref,
    prop,
    high,
    low,
    refl,
    asc,
    arriving,
    outgoing,
    passed,
    spots,
    total,
    shares,
    load_sem,
    wave_sem,
    block_sem,
    send_sem,
    recv_sem,
    give_sem,
    take_sem,
    go_sem,
    land_sem,
    onward_sem,
):
    level = lax.axis_index("depth")
    rate = lax.axis_index("freq")
    last = levels - 1
    shots, nodes = arriving.shape[2], arriving.shape[3]
    rows = shots // parts
    blocks = block_sem.shape[0]
    deep = nodes // blocks

    def block_load(k):
        return pltpu.make_async_copy(prop_hbm.at[:, pl.ds(k * deep, deep)], prop.at[:, pl.ds(k * deep, deep)], block_sem.at[k])

    def wave_load(t):
        return pltpu.make_async_copy(asc_hbm.at[t], asc.at[t], wave_sem.at[t])

    loads = [
        pltpu.make_async_copy(refl_hbm, refl, load_sem.at[0]),
        pltpu.make_async_copy(first_hbm, arriving.at[0], load_sem.at[1]),
        pltpu.make_async_copy(spots_hbm, spots, load_sem.at[2]),
    ]
    barrier = pltpu.get_barrier_semaphore()

    line, spot = level // RUN, lax.rem(level, RUN)
    lines = levels // RUN
    first = (spot == 0) & (level > 0)
    long = (spot == RUN - 1) & (level < last)
    near = (spot == NEAR) & (line < lines - 1)
    side = (spot == RUN - 2) & (line > 0)
    plain = (level < last) & (spot != RUN - 1)

    def ready(there):
        pl.semaphore_signal(barrier, inc=1, device_id={"depth": there}, device_id_type=MESH)

    @pl.when(spot > 0)
    def _():
        ready(level - 1)

    @pl.when(first)
    def _():
        ready(level - RUN + NEAR)
        ready(level + RUN - 2)

    @pl.when(near)
    def _():
        ready(level + RUN - 1 - NEAR)

    @pl.when(side)
    def _():
        ready(level - RUN + 1)

    for k in range(blocks):
        block_load(k).start()
    for load in loads:
        load.start()
    wave_load(0).start()

    home = lax.rem(level, rates)
    hub = level == last
    inside = hub & (home == rate)

    @pl.when(jnp.logical_not(inside))
    def _():
        pl.semaphore_signal(barrier, inc=1, device_id={"depth": last, "freq": home}, device_id_type=MESH)

    for k in range(blocks):
        block_load(k).wait()
        at = pl.ds(k * deep, deep)
        for part in range(2):
            whole = prop[part, at]
            top = whole.astype(jnp.bfloat16)
            high[at, part * nodes : (part + 1) * nodes] = top
            low[at, part * nodes : (part + 1) * nodes] = (whole - top.astype(jnp.float32)).astype(jnp.bfloat16)
    for load in loads:
        load.wait()
    wave_load(0).wait()
    for t in range(1, TICKS):
        wave_load(t).start()

    total[...] = jnp.zeros_like(total)

    def admit():
        @pl.when(level < last)
        def _():
            pl.semaphore_wait(barrier, 1 + jnp.where(long | near | side, 1, 0))

        @pl.when(hub)
        def _():
            pl.semaphore_wait(barrier, levels - jnp.where(inside, 1, 0))

            def release(i, carry):
                there, which = (i // rates) * rates + rate, lax.rem(i, rates)

                @pl.when(jnp.logical_or(there != level, which != rate))
                def _():
                    pl.semaphore_signal(go_sem, inc=1, device_id={"depth": there, "freq": which}, device_id_type=MESH)

                return carry

            lax.fori_loop(0, levels, release, 0)

    def passing(t, c):
        return pltpu.make_async_remote_copy(
            src_ref=outgoing.at[t, :, pl.ds(c * rows, rows)],
            dst_ref=arriving.at[t + 1, :, pl.ds(c * rows, rows)],
            send_sem=send_sem.at[t, c],
            recv_sem=recv_sem.at[t, c],
            device_id={"depth": lax.rem(level + 1, levels)},
            device_id_type=MESH,
        )

    size = rows // PIECES

    def share(which, t):
        count = SHARES[t][0]
        for k in range(1, lines - 1):
            count = jnp.where(which == k, SHARES[t][k], count)
        return count

    def piece(t, c, p):
        at = pl.ds(c * rows + p * size, size)
        return pltpu.make_async_remote_copy(
            src_ref=outgoing.at[t, :, at],
            dst_ref=passed.at[t, :, at],
            send_sem=send_sem.at[t, c],
            recv_sem=land_sem.at[t, c, p],
            device_id={"depth": jnp.where(long, jnp.where(p < share(line, t), level - RUN + 1 + NEAR, level + RUN - 1), level)},
            device_id_type=MESH,
        )

    def onward(t, c, p):
        at = pl.ds(c * rows + p * size, size)
        return pltpu.make_async_remote_copy(
            src_ref=passed.at[t, :, at],
            dst_ref=arriving.at[t + 1, :, at],
            send_sem=onward_sem.at[t, c, p],
            recv_sem=recv_sem.at[t, c],
            device_id={"depth": jnp.where(near, level + RUN - NEAR, jnp.where(side, level - RUN + 2, level))},
            device_id_type=MESH,
        )

    def carried(t, p):
        return (near & (p < share(line, t))) | (side & (p >= share(line - 1, t)))

    def send(t, c):
        @pl.when(plain)
        def _():
            passing(t, c).start()

        @pl.when(long)
        def _():
            for p in range(PIECES):
                piece(t, c, p).start()

    def relay(t, c):
        @pl.when(near | side)
        def _():
            for p in range(PIECES):

                @pl.when(carried(t, p))
                def _():
                    piece(t, c, p).wait_recv()
                    onward(t, c, p).start()

    def arrive(t, c):
        if t > 0:

            @pl.when(level > 0)
            def _():
                passing(t - 1, c).wait_recv()

    def correlate(t, c):
        at = pl.ds(c * rows, rows)
        total[...] += jnp.sum((arriving[t, :, at] * asc[t, :, at]).reshape(2 * rows // 8, 8, nodes), axis=0)

    def propagate(t, c):
        at = pl.ds(c * rows, rows)
        mixed = (arriving[t, :, at] + refl[...] * asc[t, :, at]).reshape(2 * rows, nodes)
        top = mixed.astype(jnp.bfloat16)
        rest = (mixed - top.astype(jnp.float32)).astype(jnp.bfloat16)
        both = jnp.concatenate([top, rest], axis=0)
        wide = jnp.dot(both, high[...], preferred_element_type=jnp.float32)
        wide = wide[: 2 * rows] + wide[2 * rows :] + jnp.dot(top, low[...], preferred_element_type=jnp.float32)
        result = outgoing.at[t] if t < TICKS - 1 else leaving_ref
        result[0, at] = wide[:rows, :nodes] - wide[rows:, nodes:]
        result[1, at] = wide[:rows, nodes:] + wide[rows:, :nodes]

    for c in range(parts):
        propagate(0, c)
        if c == 0:
            admit()
        send(0, c)
        correlate(0, c)

    for t in range(TICKS - 1):
        if t > 0:
            wave_load(t).wait()
        for c in range(parts if t > 0 else 0):
            if t == 1:
                relay(0, c)
            arrive(t, c)
            propagate(t, c)
            send(t, c)
            correlate(t, c)
            if t > 1:
                relay(t, c)
        if t == 1:
            for c in range(parts):
                relay(1, c)
        if t == 0:

            @pl.when(level == 0)
            def _():
                column = lax.broadcasted_iota(jnp.int32, (shots, nodes), 1)
                turned = jnp.transpose(spots[...].astype(jnp.float32)).astype(jnp.int32)
                for u in range(TICKS - 1):
                    hit = (column == turned[:, u : u + 1]).astype(jnp.float32)
                    arriving[u + 1, 0] = hit * pulse[0:1, u : u + 1]
                    arriving[u + 1, 1] = hit * pulse[1:2, u : u + 1]

    t = TICKS - 1
    wave_load(t).wait()
    for c in range(parts - 1):
        arrive(t, c)
        correlate(t, c)
        propagate(t, c)
    arrive(t, parts - 1)
    correlate(t, parts - 1)

    half = nodes // rates
    per = 128 // half
    for tile in range(nodes // 128):
        shares[rates + tile] = total[:, tile * 128 : (tile + 1) * 128]

    def give(away):
        other = lax.rem(rate + away, rates)
        return pltpu.make_async_remote_copy(
            src_ref=shares.at[rates + other // per],
            dst_ref=shares.at[away],
            send_sem=give_sem.at[away],
            recv_sem=take_sem.at[away],
            device_id={"freq": other},
            device_id_type=MESH,
        )

    @pl.when(jnp.logical_not(inside))
    def _():
        pl.semaphore_wait(go_sem, 1)

    for away in range(1, rates):
        give(away).start()

    propagate(t, parts - 1)

    @pl.when(level < last)
    def _():
        for u in range(TICKS - 1):
            for c in range(parts):
                passing(u, c).wait_send()

    @pl.when(near | side)
    def _():
        for u in range(TICKS - 1):
            for p in range(PIECES):

                @pl.when(carried(u, p))
                def _():
                    for c in range(parts):
                        onward(u, c, p).wait_send()

    summed = shares[rates + rate // per]
    for away in range(1, rates):
        give(away).wait_recv()
        summed += shares[away]
    row = jnp.sum(summed, axis=0, keepdims=True) * (1.0 / math.sqrt(shots * TICKS))
    place = lax.rem(rate, per)
    mine = row[:, :half]
    for k in range(1, per):
        mine = jnp.where(place == k, row[:, k * half : (k + 1) * half], mine)
    grad_ref[...] = mine
    for away in range(1, rates):
        give(away).wait_send()


def deliver(panel_ref, row_ref, panel_out, row_out, sems):
    copies = [
        pltpu.make_async_copy(panel_ref, panel_out, sems.at[0]),
        pltpu.make_async_copy(row_ref, row_out, sems.at[1]),
    ]
    for copy in copies:
        copy.start()
    for copy in copies:
        copy.wait()


def local(levels, rates, prop, refl, asc, first, spots, pulse):
    shots, nodes = first.shape[3], first.shape[4]
    parts = 3
    prop = prop.reshape(2, nodes, nodes)
    asc = asc.reshape(TICKS, 2, shots, nodes)
    first = first.reshape(2, shots, nodes)
    pulse = pulse.reshape(TICKS - 1, 2).T
    prop, refl, asc, first, spots, pulse = (pltpu.with_memory_space_constraint(x, pltpu.HBM) for x in (prop, refl, asc, first, spots, pulse))
    leaving, grad = pl.pallas_call(
        functools.partial(kernel, levels, rates, parts),
        out_shape=(
            jax.ShapeDtypeStruct((2, shots, nodes), jnp.float32),
            jax.ShapeDtypeStruct((1, nodes // rates), jnp.float32),
        ),
        in_specs=[pl.BlockSpec(memory_space=pltpu.HBM)] * 5 + [pl.BlockSpec(memory_space=pltpu.VMEM)],
        out_specs=(pl.BlockSpec(memory_space=pltpu.VMEM), pl.BlockSpec(memory_space=pltpu.VMEM)),
        scratch_shapes=[
            pltpu.VMEM((2, nodes, nodes), jnp.float32),
            pltpu.VMEM((nodes, 2 * nodes), jnp.bfloat16),
            pltpu.VMEM((nodes, 2 * nodes), jnp.bfloat16),
            pltpu.VMEM((1, nodes), jnp.float32),
            pltpu.VMEM((TICKS, 2, shots, nodes), jnp.float32),
            pltpu.VMEM((TICKS, 2, shots, nodes), jnp.float32),
            pltpu.VMEM((TICKS - 1, 2, shots, nodes), jnp.float32),
            pltpu.VMEM((TICKS - 1, 2, shots, nodes), jnp.float32),
            pltpu.VMEM((TICKS - 1, shots), jnp.int32),
            pltpu.VMEM((8, nodes), jnp.float32),
            pltpu.VMEM((rates + nodes // 128, 8, 128), jnp.float32),
            pltpu.SemaphoreType.DMA((3,)),
            pltpu.SemaphoreType.DMA((TICKS,)),
            pltpu.SemaphoreType.DMA((4,)),
            pltpu.SemaphoreType.DMA((TICKS - 1, parts)),
            pltpu.SemaphoreType.DMA((TICKS - 1, parts)),
            pltpu.SemaphoreType.DMA((rates,)),
            pltpu.SemaphoreType.DMA((rates,)),
            pltpu.SemaphoreType.REGULAR,
            pltpu.SemaphoreType.DMA((TICKS - 1, parts, PIECES)),
            pltpu.SemaphoreType.DMA((TICKS - 1, parts, PIECES)),
        ],
        compiler_params=pltpu.CompilerParams(collective_id=0, has_side_effects=True, vmem_limit_bytes=32 << 20),
    )(prop, refl, asc, first, spots, pulse)
    leaving, grad = pl.pallas_call(
        deliver,
        out_shape=(
            jax.ShapeDtypeStruct(leaving.shape, jnp.float32),
            jax.ShapeDtypeStruct(grad.shape, jnp.float32),
        ),
        in_specs=[pl.BlockSpec(memory_space=pltpu.VMEM)] * 2,
        out_specs=(pl.BlockSpec(memory_space=pltpu.HBM), pl.BlockSpec(memory_space=pltpu.HBM)),
        scratch_shapes=[pltpu.SemaphoreType.DMA((2,))],
        compiler_params=pltpu.CompilerParams(vmem_limit_bytes=16 << 20),
        name="deliver",
    )(leaving, grad)
    return leaving[None, None], grad


def solution(mesh):
    placed = (
        P("freq", "depth", None, None, None),
        P("depth", None),
        P("freq", "depth", None, None, None, None),
        P("freq", "depth", None, None, None),
        P(),
        P("freq", None, None),
    )
    return jax.shard_map(
        functools.partial(local, mesh.shape["depth"], mesh.shape["freq"]),
        mesh=mesh,
        in_specs=placed,
        out_specs=(P("freq", "depth", None, None, None), P("depth", "freq")),
        check_vma=False,
    )
```

```python
import functools
import math

import jax
import jax.numpy as jnp
from jax import lax
from jax.experimental import pallas as pl
from jax.experimental.pallas import tpu as pltpu
from jax.sharding import PartitionSpec as P

TICKS = 5
RUN = 16
NEAR = 10
SHARES = ((4, 3, 1), (3, 2, 1), (3, 2, 1), (2, 1, 1))
PIECES = 4
MESH = pl.DeviceIdType.MESH


def kernel(
    levels,
    rates,
    parts,
    prop_hbm,
    refl_hbm,
    asc_hbm,
    first_hbm,
    spots_hbm,
    pulse,
    leaving_ref,
    grad_ref,
    prop,
    high,
    low,
    refl,
    asc,
    arriving,
    outgoing,
    passed,
    spots,
    total,
    shares,
    load_sem,
    wave_sem,
    block_sem,
    send_sem,
    recv_sem,
    give_sem,
    take_sem,
    go_sem,
    land_sem,
    onward_sem,
):
    level = lax.axis_index("depth")
    rate = lax.axis_index("freq")
    last = levels - 1
    shots, nodes = arriving.shape[2], arriving.shape[3]
    rows = shots // parts
    blocks = block_sem.shape[0]
    deep = nodes // blocks

    def block_load(k):
        return pltpu.make_async_copy(prop_hbm.at[:, pl.ds(k * deep, deep)], prop.at[:, pl.ds(k * deep, deep)], block_sem.at[k])

    def wave_load(t):
        return pltpu.make_async_copy(asc_hbm.at[t], asc.at[t], wave_sem.at[t])

    loads = [
        pltpu.make_async_copy(refl_hbm, refl, load_sem.at[0]),
        pltpu.make_async_copy(first_hbm, arriving.at[0], load_sem.at[1]),
        pltpu.make_async_copy(spots_hbm, spots, load_sem.at[2]),
    ]
    barrier = pltpu.get_barrier_semaphore()

    line, spot = level // RUN, lax.rem(level, RUN)
    lines = levels // RUN
    first = (spot == 0) & (level > 0)
    long = (spot == RUN - 1) & (level < last)
    near = (spot == NEAR) & (line < lines - 1)
    side = (spot == RUN - 2) & (line > 0)
    plain = (level < last) & (spot != RUN - 1)

    def ready(there):
        pl.semaphore_signal(barrier, inc=1, device_id={"depth": there}, device_id_type=MESH)

    @pl.when(spot > 0)
    def _():
        ready(level - 1)

    @pl.when(first)
    def _():
        ready(level - RUN + NEAR)
        ready(level + RUN - 2)

    @pl.when(near)
    def _():
        ready(level + RUN - 1 - NEAR)

    @pl.when(side)
    def _():
        ready(level - RUN + 1)

    for k in range(blocks):
        block_load(k).start()
    for load in loads:
        load.start()
    wave_load(0).start()

    home = lax.rem(level, rates)
    hub = level == last
    inside = hub & (home == rate)

    @pl.when(jnp.logical_not(inside))
    def _():
        pl.semaphore_signal(barrier, inc=1, device_id={"depth": last, "freq": home}, device_id_type=MESH)

    for k in range(blocks):
        block_load(k).wait()
        at = pl.ds(k * deep, deep)
        for part in range(2):
            whole = prop[part, at]
            top = whole.astype(jnp.bfloat16)
            high[at, part * nodes : (part + 1) * nodes] = top
            low[at, part * nodes : (part + 1) * nodes] = (whole - top.astype(jnp.float32)).astype(jnp.bfloat16)
    for load in loads:
        load.wait()
    wave_load(0).wait()
    for t in range(1, TICKS):
        wave_load(t).start()

    total[...] = jnp.zeros_like(total)

    def admit():
        @pl.when(level < last)
        def _():
            pl.semaphore_wait(barrier, 1 + jnp.where(long | near | side, 1, 0))

        @pl.when(hub)
        def _():
            pl.semaphore_wait(barrier, levels - jnp.where(inside, 1, 0))

            def release(i, carry):
                there, which = (i // rates) * rates + rate, lax.rem(i, rates)

                @pl.when(jnp.logical_or(there != level, which != rate))
                def _():
                    pl.semaphore_signal(go_sem, inc=1, device_id={"depth": there, "freq": which}, device_id_type=MESH)

                return carry

            lax.fori_loop(0, levels, release, 0)

    def passing(t, c):
        return pltpu.make_async_remote_copy(
            src_ref=outgoing.at[t, :, pl.ds(c * rows, rows)],
            dst_ref=arriving.at[t + 1, :, pl.ds(c * rows, rows)],
            send_sem=send_sem.at[t, c],
            recv_sem=recv_sem.at[t, c],
            device_id={"depth": lax.rem(level + 1, levels)},
            device_id_type=MESH,
        )

    size = rows // PIECES

    def share(which, t):
        count = SHARES[t][0]
        for k in range(1, lines - 1):
            count = jnp.where(which == k, SHARES[t][k], count)
        return count

    def piece(t, c, p):
        at = pl.ds(c * rows + p * size, size)
        return pltpu.make_async_remote_copy(
            src_ref=outgoing.at[t, :, at],
            dst_ref=passed.at[t, :, at],
            send_sem=send_sem.at[t, c],
            recv_sem=land_sem.at[t, c, p],
            device_id={"depth": jnp.where(long, jnp.where(p < share(line, t), level - RUN + 1 + NEAR, level + RUN - 1), level)},
            device_id_type=MESH,
        )

    def onward(t, c, p):
        at = pl.ds(c * rows + p * size, size)
        return pltpu.make_async_remote_copy(
            src_ref=passed.at[t, :, at],
            dst_ref=arriving.at[t + 1, :, at],
            send_sem=onward_sem.at[t, c, p],
            recv_sem=recv_sem.at[t, c],
            device_id={"depth": jnp.where(near, level + RUN - NEAR, jnp.where(side, level - RUN + 2, level))},
            device_id_type=MESH,
        )

    def carried(t, p):
        return (near & (p < share(line, t))) | (side & (p >= share(line - 1, t)))

    def send(t, c):
        @pl.when(plain)
        def _():
            passing(t, c).start()

        @pl.when(long)
        def _():
            for p in range(PIECES):
                piece(t, c, p).start()

    def relay(t, c):
        @pl.when(near | side)
        def _():
            for p in range(PIECES):

                @pl.when(carried(t, p))
                def _():
                    piece(t, c, p).wait_recv()
                    onward(t, c, p).start()

    def arrive(t, c):
        if t > 0:

            @pl.when(level > 0)
            def _():
                passing(t - 1, c).wait_recv()

    def correlate(t, c):
        at = pl.ds(c * rows, rows)
        total[...] += jnp.sum((arriving[t, :, at] * asc[t, :, at]).reshape(2 * rows // 8, 8, nodes), axis=0)

    def propagate(t, c):
        at = pl.ds(c * rows, rows)
        mixed = (arriving[t, :, at] + refl[...] * asc[t, :, at]).reshape(2 * rows, nodes)
        top = mixed.astype(jnp.bfloat16)
        rest = (mixed - top.astype(jnp.float32)).astype(jnp.bfloat16)
        both = jnp.concatenate([top, rest], axis=0)
        wide = jnp.dot(both, high[...], preferred_element_type=jnp.float32)
        wide = wide[: 2 * rows] + wide[2 * rows :] + jnp.dot(top, low[...], preferred_element_type=jnp.float32)
        result = outgoing.at[t] if t < TICKS - 1 else leaving_ref
        result[0, at] = wide[:rows, :nodes] - wide[rows:, nodes:]
        result[1, at] = wide[:rows, nodes:] + wide[rows:, :nodes]

    for c in range(parts):
        propagate(0, c)
        if c == 0:
            admit()
        send(0, c)
        correlate(0, c)

    for t in range(TICKS - 1):
        if t > 0:
            wave_load(t).wait()
        for c in range(parts if t > 0 else 0):
            if t == 1:
                relay(0, c)
            arrive(t, c)
            propagate(t, c)
            send(t, c)
            correlate(t, c)
            if t > 1:
                relay(t, c)
        if t == 1:
            for c in range(parts):
                relay(1, c)
        if t == 0:

            @pl.when(level == 0)
            def _():
                column = lax.broadcasted_iota(jnp.int32, (shots, nodes), 1)
                turned = jnp.transpose(spots[...].astype(jnp.float32)).astype(jnp.int32)
                for u in range(TICKS - 1):
                    hit = (column == turned[:, u : u + 1]).astype(jnp.float32)
                    arriving[u + 1, 0] = hit * pulse[0:1, u : u + 1]
                    arriving[u + 1, 1] = hit * pulse[1:2, u : u + 1]

    t = TICKS - 1
    wave_load(t).wait()
    for c in range(parts - 1):
        arrive(t, c)
        correlate(t, c)
        propagate(t, c)
    arrive(t, parts - 1)
    correlate(t, parts - 1)

    half = nodes // rates
    per = 128 // half
    for tile in range(nodes // 128):
        shares[rates + tile] = total[:, tile * 128 : (tile + 1) * 128]

    def give(away):
        other = lax.rem(rate + away, rates)
        return pltpu.make_async_remote_copy(
            src_ref=shares.at[rates + other // per],
            dst_ref=shares.at[away],
            send_sem=give_sem.at[away],
            recv_sem=take_sem.at[away],
            device_id={"freq": other},
            device_id_type=MESH,
        )

    @pl.when(jnp.logical_not(inside))
    def _():
        pl.semaphore_wait(go_sem, 1)

    for away in (*range(1, rates, 2), *range(2, rates, 2)):
        give(away).start()

    propagate(t, parts - 1)

    @pl.when(level < last)
    def _():
        for u in range(TICKS - 1):
            for c in range(parts):
                passing(u, c).wait_send()

    @pl.when(near | side)
    def _():
        for u in range(TICKS - 1):
            for p in range(PIECES):

                @pl.when(carried(u, p))
                def _():
                    for c in range(parts):
                        onward(u, c, p).wait_send()

    summed = shares[rates + rate // per]
    for away in range(1, rates):
        give(away).wait_recv()
        summed += shares[away]
    row = jnp.sum(summed, axis=0, keepdims=True) * (1.0 / math.sqrt(shots * TICKS))
    place = lax.rem(rate, per)
    mine = row[:, :half]
    for k in range(1, per):
        mine = jnp.where(place == k, row[:, k * half : (k + 1) * half], mine)
    grad_ref[...] = mine
    for away in range(1, rates):
        give(away).wait_send()


def deliver(panel_ref, row_ref, panel_out, row_out, sems):
    copies = [
        pltpu.make_async_copy(panel_ref, panel_out, sems.at[0]),
        pltpu.make_async_copy(row_ref, row_out, sems.at[1]),
    ]
    for copy in copies:
        copy.start()
    for copy in copies:
        copy.wait()


def local(levels, rates, prop, refl, asc, first, spots, pulse):
    shots, nodes = first.shape[3], first.shape[4]
    parts = 3
    prop = prop.reshape(2, nodes, nodes)
    asc = asc.reshape(TICKS, 2, shots, nodes)
    first = first.reshape(2, shots, nodes)
    pulse = pulse.reshape(TICKS - 1, 2).T
    prop, refl, asc, first, spots, pulse = (pltpu.with_memory_space_constraint(x, pltpu.HBM) for x in (prop, refl, asc, first, spots, pulse))
    leaving, grad = pl.pallas_call(
        functools.partial(kernel, levels, rates, parts),
        out_shape=(
            jax.ShapeDtypeStruct((2, shots, nodes), jnp.float32),
            jax.ShapeDtypeStruct((1, nodes // rates), jnp.float32),
        ),
        in_specs=[pl.BlockSpec(memory_space=pltpu.HBM)] * 5 + [pl.BlockSpec(memory_space=pltpu.VMEM)],
        out_specs=(pl.BlockSpec(memory_space=pltpu.VMEM), pl.BlockSpec(memory_space=pltpu.VMEM)),
        scratch_shapes=[
            pltpu.VMEM((2, nodes, nodes), jnp.float32),
            pltpu.VMEM((nodes, 2 * nodes), jnp.bfloat16),
            pltpu.VMEM((nodes, 2 * nodes), jnp.bfloat16),
            pltpu.VMEM((1, nodes), jnp.float32),
            pltpu.VMEM((TICKS, 2, shots, nodes), jnp.float32),
            pltpu.VMEM((TICKS, 2, shots, nodes), jnp.float32),
            pltpu.VMEM((TICKS - 1, 2, shots, nodes), jnp.float32),
            pltpu.VMEM((TICKS - 1, 2, shots, nodes), jnp.float32),
            pltpu.VMEM((TICKS - 1, shots), jnp.int32),
            pltpu.VMEM((8, nodes), jnp.float32),
            pltpu.VMEM((rates + nodes // 128, 8, 128), jnp.float32),
            pltpu.SemaphoreType.DMA((3,)),
            pltpu.SemaphoreType.DMA((TICKS,)),
            pltpu.SemaphoreType.DMA((4,)),
            pltpu.SemaphoreType.DMA((TICKS - 1, parts)),
            pltpu.SemaphoreType.DMA((TICKS - 1, parts)),
            pltpu.SemaphoreType.DMA((rates,)),
            pltpu.SemaphoreType.DMA((rates,)),
            pltpu.SemaphoreType.REGULAR,
            pltpu.SemaphoreType.DMA((TICKS - 1, parts, PIECES)),
            pltpu.SemaphoreType.DMA((TICKS - 1, parts, PIECES)),
        ],
        compiler_params=pltpu.CompilerParams(collective_id=0, has_side_effects=True, vmem_limit_bytes=32 << 20),
    )(prop, refl, asc, first, spots, pulse)
    leaving, grad = pl.pallas_call(
        deliver,
        out_shape=(
            jax.ShapeDtypeStruct(leaving.shape, jnp.float32),
            jax.ShapeDtypeStruct(grad.shape, jnp.float32),
        ),
        in_specs=[pl.BlockSpec(memory_space=pltpu.VMEM)] * 2,
        out_specs=(pl.BlockSpec(memory_space=pltpu.HBM), pl.BlockSpec(memory_space=pltpu.HBM)),
        scratch_shapes=[pltpu.SemaphoreType.DMA((2,))],
        compiler_params=pltpu.CompilerParams(vmem_limit_bytes=16 << 20),
        name="deliver",
    )(leaving, grad)
    return leaving[None, None], grad


def solution(mesh):
    placed = (
        P("freq", "depth", None, None, None),
        P("depth", None),
        P("freq", "depth", None, None, None, None),
        P("freq", "depth", None, None, None),
        P(),
        P("freq", None, None),
    )
    return jax.shard_map(
        functools.partial(local, mesh.shape["depth"], mesh.shape["freq"]),
        mesh=mesh,
        in_specs=placed,
        out_specs=(P("freq", "depth", None, None, None), P("depth", "freq")),
        check_vma=False,
    )
```
